32 devices in a mesh: replica: 4 (over y, x), fsdp: 8 (over z, core).
Axes of the slice: x: 2, y: 2, z: 4, core: 2. Of those that a mesh axis runs over, the one named last changes fastest.
Arguments:
- token_ids: int32 [4096], P(('replica', 'fsdp')), may hold values from 0 to 128000, as said below
- inputs: bfloat16 [4096, 8192], P(('replica', 'fsdp')), may hold values from -6 to 6
- key_cotangent: bfloat16 [4096, 768], P(('replica', 'fsdp')), may hold values from -6 to 6
- key_weight: float32 [4, 8192, 768], P('replica', 'fsdp'), may hold values from -0.0625 to 0.0625
- adam_m: float32 [4, 8192, 768], P('replica', 'fsdp'), may hold values from -0.5 to 0.5
- adam_v: float32 [4, 8192, 768], P('replica', 'fsdp'), may hold values from 9.765625e-05 to 0.009765625
- frag_local: float32 [4, 3, 8192, 512], P('replica', None, 'fsdp'), may hold values from -0.0625 to 0.0625
- frag_global: float32 [4, 8192, 512], P('replica', 'fsdp'), may hold values from -0.0625 to 0.0625
- outer_mom: float32 [4, 8192, 512], P('replica', 'fsdp'), may hold values from -0.15625 to 0.15625
- owner: int32 [8], P('fsdp'), may hold values from 0 to 3
- fragment: int32 [4], P('replica'), may hold values from 0 to 2
Outputs:
- input_cotangent: bfloat16 [4096, 8192], P(('replica', 'fsdp'))
- new_weight: float32 [4, 8192, 768], P('replica', 'fsdp')
- new_m: float32 [4, 8192, 768], P('replica', 'fsdp')
- new_v: float32 [4, 8192, 768], P('replica', 'fsdp')
- synced: float32 [4, 8192, 512], P('replica', 'fsdp')
- new_outer_mom: float32 [4, 8192, 512], P('replica', 'fsdp')
The draws below stay inside these ranges and needn't reach their ends.
Inputs may be any that keep to these rules, and one draw needn't show every extreme that they name: `token_ids`: token 0 of every replica's sequence of 1024 tokens is 128000, the id that begins a document; the same id begins every later document.
All inputs are finite; a program needn't handle non-finite values.
Results may differ from the reference program's by a relative error of at most 0.0095.
Values may be sent and summed in bfloat16 or wider, within the bound.
A program may use at most 128 MiB of HBM per device.

```python
import math
import jax
import jax.numpy as jnp
from jax import lax

D = 8192
HEAD = 128
FW = 512
NFRAG = 3
TOK_DEV = 128
KVW = 768
SEQ = 1024
REPLICAS = 4
TOKENS = 4096
N_FSDP = 8


def draw_token_ids(key, part):
    word_key = jax.random.fold_in(key, 11)
    start_key = jax.random.fold_in(key, 12)
    word_ids = jax.random.randint(word_key, (TOKENS,), 0, 128000, dtype=jnp.int32)
    start_marks = jax.random.randint(start_key, (TOKENS,), 0, 4 * TOK_DEV, dtype=jnp.int32)
    token_index = jnp.arange(TOKENS, dtype=jnp.int32)
    is_first = token_index % SEQ == 0
    return jnp.where(is_first | (start_marks == 0), 128000, word_ids).astype(jnp.int32)


def plant(values, own_key, least, high):
    index_at = [jax.random.randint(jax.random.fold_in(own_key, axis), (), 0, length) for axis, length in enumerate(values.shape)]
    longest = values.shape.index(max(values.shape))
    beside = index_at[:longest] + [(index_at[longest] + 1) % values.shape[longest]] + index_at[longest + 1:]
    return values.at[tuple(index_at)].set(least).at[tuple(beside)].set(high)


def strengthened(drawn, own_key, source, target, parts, factor):
    owner, partner = [(jnp.arange(drawn.shape[dim]) // (drawn.shape[dim] // parts)).reshape([-1 if axis == dim else 1 for axis in range(drawn.ndim)]) for dim in (source, target)]
    chosen = jax.random.permutation(own_key, parts)[partner]
    strong = (owner == chosen) | (owner == (partner + parts // 2) % parts)
    return jnp.where(strong, factor * drawn, drawn)


def block_levels(own_key, extent, cuts, low, largest):
    factor_of, own = 1.0, jax.random.fold_in(own_key, 6)
    for axis_at, shards_of in cuts:
        draws = jnp.exp(jax.random.uniform(jax.random.fold_in(own, axis_at), (shards_of,), jnp.float32, low / len(cuts), largest / len(cuts)))
        factor_of = factor_of * jnp.repeat(draws, extent[axis_at] // shards_of).reshape([-1 if axis == axis_at else 1 for axis in range(len(extent))])
    return factor_of


def bell_draw(key, dims, spread, limit, shards=(), kind=jnp.bfloat16):
    array = jax.random.normal(key, dims, jnp.float32) * spread
    if len(shards) > 0:
        array = block_levels(key, dims, shards, -0.22, 0.18) * array
    return jnp.clip(array, min=-limit, max=limit).astype(kind)


def noise_with(rng, dims, scale, reach, pieces, heavy, kind=jnp.bfloat16):
    drawn = scale * jax.random.normal(rng, dims, jnp.float32)
    if pieces:
        drawn = drawn * block_levels(rng, dims, pieces, -0.22, 0.18)
    return jnp.clip(strengthened(drawn, jax.random.fold_in(rng, 3), *heavy), -reach, reach).astype(kind)


def setup_inputs(seed: int = 0) -> dict:
    splits = jax.random.split(jax.random.key(seed), 12)
    token_ids = draw_token_ids(jax.random.fold_in(splits[11], 71), 0)
    inputs = noise_with(splits[1], (TOKENS, D), 1.0, 6.0, ((0, 32),), (0, 1, 32, 2.75))
    key_cotangent = bell_draw(splits[2], (TOKENS, KVW), 1.0, 6.0, ((0, 32),))
    key_weight = bell_draw(splits[3], (REPLICAS, D, KVW), D ** -0.5, 0.0625, ((0, 4), (1, 8)), jnp.float32)
    adam_m = bell_draw(splits[4], (REPLICAS, D, KVW), (SEQ ** -0.5), 0.5, ((0, 4), (1, 8)), jnp.float32)
    adam_v = jnp.clip(jnp.exp(math.log(0.009765625) - 4.6051702 * jax.random.uniform(splits[5], (REPLICAS, D, KVW), jnp.float32) ** block_levels(splits[5], (REPLICAS, D, KVW), ((0, 4), (1, 8)), -0.2, 0.2)), 9.765625145519152e-05, 0.009765625)
    frag_local = bell_draw(splits[6], (REPLICAS, NFRAG, D, FW), D ** -0.5, 0.0625, ((0, 4), (2, 8)), jnp.float32)
    frag_global = bell_draw(splits[7], (REPLICAS, D, FW), D ** -0.5, 0.0625, ((0, 4), (1, 8)), jnp.float32)
    outer_mom = bell_draw(splits[8], (REPLICAS, D, FW), (D ** -0.5), 0.15625, ((0, 4), (1, 8)), jnp.float32)
    owner = plant(jax.random.randint(splits[9], (N_FSDP,), 0, REPLICAS), jax.random.fold_in(splits[9], 1), 0, REPLICAS - 1).astype(jnp.int32)
    fragment = plant(jax.random.randint(splits[10], (REPLICAS,), 0, NFRAG), jax.random.fold_in(splits[10], 1), 0, NFRAG - 1).astype(jnp.int32)
    return {"token_ids": token_ids, "inputs": inputs, "key_cotangent": key_cotangent, "key_weight": key_weight, "adam_m": adam_m, "adam_v": adam_v, "frag_local": frag_local, "frag_global": frag_global, "outer_mom": outer_mom, "owner": owner, "fragment": fragment}


begin_token = 128000
rope_base = 500000.0
beta_one = 0.9
beta_two = 0.95
adam_lr = 0.001
adam_eps = 1e-08
adam_step = 10.0
weight_decay = 0.1
outer_lr = 0.7
outer_momentum = 0.9

def unrotate(cotangent, positions):
    row_count = cotangent.shape[0]
    head_count = cotangent.shape[1] // HEAD
    half_head = HEAD // 2
    frequency = jnp.float32(rope_base) ** (-(jnp.arange(half_head, dtype=jnp.float32) * (2.0 / HEAD)))
    angles = positions.astype(jnp.float32)[:, None] * frequency[None, :]
    cosine = jnp.cos(angles)[:, None, :]
    sine_part = jnp.sin(angles)[:, None, :]
    per_head = cotangent.astype(jnp.float32).reshape(row_count, head_count, HEAD)
    front_half = per_head[..., :half_head]
    back_half = per_head[..., half_head:]
    turned = jnp.concatenate([front_half * cosine + back_half * sine_part, back_half * cosine - front_half * sine_part], axis=-1)
    return turned.reshape(row_count, head_count * HEAD).astype(jnp.bfloat16)

def doc_positions(sequence_ids):
    token_index = jnp.arange(sequence_ids.shape[0], dtype=jnp.int32)
    starts = jnp.where(sequence_ids == begin_token, token_index, -1)
    return token_index - lax.cummax(starts, axis=0)

def reference(token_ids, inputs, key_cotangent, key_weight, adam_m, adam_v, frag_local, frag_global, outer_mom, owner, fragment):
    replica_ids = token_ids.reshape(REPLICAS, SEQ)
    positions = jax.vmap(doc_positions)(replica_ids).reshape(REPLICAS * SEQ)
    key_grad = unrotate(key_cotangent, positions).reshape(REPLICAS, SEQ, -1)
    weight_bf = key_weight.astype(jnp.bfloat16)
    stacked = inputs.reshape(REPLICAS, SEQ, D)

    def one_replica(operands):
        rows_in, grads_in, weight_in = operands
        back_grad = lax.dot_general(grads_in, weight_in, (((1,), (1,)), ((), ())), preferred_element_type=jnp.float32).astype(jnp.bfloat16)
        input_blocks = rows_in.reshape(N_FSDP, TOK_DEV, D)
        grad_blocks = grads_in.reshape(N_FSDP, TOK_DEV, grads_in.shape[1])

        def add_block(running, block_pair):
            partial_value = lax.dot_general(block_pair[0], block_pair[1], (((0,), (0,)), ((), ())), preferred_element_type=jnp.float32)
            rounded = lax.optimization_barrier(partial_value.astype(jnp.bfloat16))
            return (running + rounded.astype(jnp.float32), None)
        summed = lax.scan(add_block, jnp.zeros((D, grads_in.shape[1]), jnp.float32), (input_blocks, grad_blocks))[0]
        return (back_grad, summed / SEQ)
    input_cotangent, weight_grad = lax.map(one_replica, (stacked, key_grad, weight_bf))
    moment_mean = beta_one * adam_m + (1.0 - beta_one) * weight_grad
    moment_square = beta_two * adam_v + (1.0 - beta_two) * weight_grad * weight_grad
    mean_hat = moment_mean / (1.0 - beta_one ** adam_step)
    square_hat = moment_square / (1.0 - beta_two ** adam_step)
    new_weight = key_weight - adam_lr * (mean_hat / (jnp.sqrt(square_hat) + adam_eps) + weight_decay * key_weight)
    slot_index = fragment.astype(jnp.int32)[:, None, None, None]
    local_slot = jnp.take_along_axis(frag_local, slot_index, axis=1)[:, 0]
    owner_rows = jnp.repeat(owner.astype(jnp.int32), D // N_FSDP)
    slot_rank = jnp.arange(REPLICAS, dtype=jnp.int32)[:, None]
    owned = (slot_rank == owner_rows[None, :])[:, :, None]
    state_global = lax.optimization_barrier(jnp.sum(jnp.where(owned, frag_global, 0.0), axis=0))
    state_mom = lax.optimization_barrier(jnp.sum(jnp.where(owned, outer_mom, 0.0), axis=0))
    outer_grad = state_global - lax.optimization_barrier(jnp.sum(local_slot, axis=0)) / REPLICAS
    mom_next = outer_momentum * state_mom + outer_grad
    synced_one = state_global - outer_lr * (outer_grad + outer_momentum * mom_next)
    synced = jnp.broadcast_to(synced_one[None], (REPLICAS, D, FW))
    new_outer_mom = jnp.where(owned, mom_next[None], outer_mom)
    return (input_cotangent.reshape(REPLICAS * SEQ, D), new_weight, moment_mean, moment_square, synced, new_outer_mom)
```

```python
import functools
import math

import jax
import jax.numpy as jnp
from jax import lax
from jax.experimental import pallas as pl
from jax.experimental.pallas import tpu as pltpu
from jax.sharding import PartitionSpec as P

HEAD = 128


begin_token = 128000
rope_base = 500000.0
beta_one = 0.9
beta_two = 0.95
adam_lr = 0.001
adam_eps = 1e-08
adam_step = 10.0
weight_decay = 0.1
outer_lr = 0.7
outer_momentum = 0.9


MESH = pl.DeviceIdType.MESH


def flip(index, mask, size):
    total, bit = 0, 1
    while bit < size:
        own, other = (index // bit) % 2, (mask // bit) % 2
        total = total + bit * (own + other - 2 * own * other)
        bit *= 2
    return total


def tail_masks(n):
    return [mask for mask in (n // 2, n // 2 + n // 4) if mask % 2 == 0] if n > 4 else []


def through(n, blocks_ref, out_ref, held, in_sem, out_sem):
    rows = blocks_ref.shape[1] // n
    spans = [slice(j * rows, (j + 1) * rows) for j in range(n)]
    arrive = [
        pltpu.make_async_copy(blocks_ref.at[:, at], held.at[:, at], in_sem.at[j])
        for j, at in enumerate(spans)
    ]
    leave = [
        pltpu.make_async_copy(held.at[:, at], out_ref.at[:, at], out_sem.at[j])
        for j, at in enumerate(spans)
    ]
    for copy in arrive:
        copy.start()
    for j in range(n):
        arrive[j].wait()
        leave[j].start()
    for copy in leave:
        copy.wait()


def put_last(n, *refs):
    masks = tail_masks(n)
    blocks, out_ref, sem = refs[1 : 1 + len(masks)], refs[-2], refs[-1]
    me = lax.axis_index("fsdp")
    rows = blocks[0].shape[1]
    copies = []
    for k, mask in enumerate(masks):
        at = pl.ds(pl.multiple_of(flip(me, mask, n) * rows, rows), rows)
        copies.append(pltpu.make_async_copy(blocks[k], out_ref.at[:, at], sem.at[k]))
    for copy in copies:
        copy.start()
    for copy in copies:
        copy.wait()


def exchange(
    n,
    replicas,
    owner_ref,
    fragment_ref,
    tok_ref,
    kc_hbm,
    x_hbm,
    w_hbm,
    local_hbm,
    global_hbm,
    mom_hbm,
    *rest,
):
    masks = tail_masks(n)
    cols_out, kg_out, sync_out, ic_out = rest[:4]
    tail_out, rest = rest[4 : 4 + len(masks)], rest[4 + len(masks) :]
    (
        kc_all,
        tok_all,
        kg_buf,
        ic_buf,
        w_buf,
        w_bf,
        local_buf,
        global_buf,
        mom_buf,
        mine,
        parts,
        own_cols,
        load_sem,
        save_sem,
        tok_send,
        tok_recv,
        kc_send_right,
        kc_send_left,
        kc_send_side,
        kc_recv,
        x_send,
        x_recv,
        ic_send,
        ic_recv,
        f_send,
        f_recv,
        g_send,
        g_recv,
    ) = rest
    me = lax.axis_index("fsdp")
    rep = lax.axis_index("replica")
    chips = n // 2
    chip, core = me // 2, me % 2
    side = me + 1 - 2 * core
    tokens, width = kc_hbm.shape
    rows = w_hbm.shape[0]
    quarter = rows // replicas
    step_rows = min(32, quarter)

    barrier = pltpu.get_barrier_semaphore()
    for d in range(1, n):
        pl.semaphore_signal(
            barrier, inc=1, device_id={"fsdp": (me + d) % n}, device_id_type=MESH
        )
    for d in range(1, replicas):
        pl.semaphore_signal(
            barrier, inc=1, device_id={"replica": (rep + d) % replicas}, device_id_type=MESH
        )

    loads = [
        pltpu.make_async_copy(local_hbm, local_buf, load_sem.at[0]),
        pltpu.make_async_copy(global_hbm, global_buf, load_sem.at[1]),
        pltpu.make_async_copy(mom_hbm, mom_buf, load_sem.at[2]),
        pltpu.make_async_copy(kc_hbm, kc_all.at[me], load_sem.at[3]),
        pltpu.make_async_copy(tok_ref, tok_all.at[me], load_sem.at[4]),
        pltpu.make_async_copy(
            x_hbm.at[:, pl.ds(pl.multiple_of(me * rows, rows), rows)], own_cols, load_sem.at[5]
        ),
        pltpu.make_async_copy(w_hbm, w_buf, load_sem.at[6]),
    ]
    for load in loads:
        load.start()
    pl.semaphore_wait(barrier, n - 1 + replicas - 1)

    def tok_copy(d):
        return pltpu.make_async_remote_copy(
            src_ref=tok_ref,
            dst_ref=tok_all.at[me],
            send_sem=tok_send.at[d],
            recv_sem=tok_recv.at[me],
            device_id={"fsdp": (me + d) % n},
            device_id_type=MESH,
        )

    def kc_copy(block, target, send_sem, first=False):
        return pltpu.make_async_remote_copy(
            src_ref=kc_hbm if first else kc_all.at[block],
            dst_ref=kc_all.at[block],
            send_sem=send_sem,
            recv_sem=kc_recv.at[block],
            device_id={"fsdp": target},
            device_id_type=MESH,
        )

    def block_of(at_chip):
        return jnp.clip(at_chip, 0, chips - 1) * 2 + core

    def right(s):
        target = jnp.minimum(me + 2, n - 1)
        return kc_copy(block_of(chip - s), target, kc_send_right.at[s], s == 0)

    def left(s):
        target = jnp.maximum(me - 2, 0)
        return kc_copy(block_of(chip + s), target, kc_send_left.at[s], s == 0)

    def goes_right(s):
        return jnp.logical_and(chip - s >= 0, chip + 1 < chips)

    def goes_left(s):
        return jnp.logical_and(chip + s < chips, chip >= 1)

    def beside(at_chip, first=False):
        at = jnp.clip(at_chip, 0, chips - 1)
        return kc_copy(at * 2 + core, side, kc_send_side.at[at], first)

    def x_copy(mask):
        peer = flip(me, mask, n)
        return pltpu.make_async_remote_copy(
            src_ref=x_hbm.at[:, pl.ds(pl.multiple_of(peer * rows, rows), rows)],
            dst_ref=cols_out.at[me],
            send_sem=x_send.at[mask],
            recv_sem=x_recv.at[me],
            device_id={"fsdp": peer},
            device_id_type=MESH,
        )

    def span_of(at):
        return pl.ds(pl.multiple_of(at * rows, rows), rows)

    def ic_copy(mask):
        peer = flip(me, mask, n)
        return pltpu.make_async_remote_copy(
            src_ref=ic_buf.at[peer],
            dst_ref=ic_out.at[:, span_of(me)],
            send_sem=ic_send.at[mask],
            recv_sem=ic_recv.at[mask],
            device_id={"fsdp": peer},
            device_id_type=MESH,
        )

    def f_copy(d):
        peer = (rep + d) % replicas
        return pltpu.make_async_remote_copy(
            src_ref=mine.at[peer],
            dst_ref=parts.at[rep],
            send_sem=f_send.at[d],
            recv_sem=f_recv.at[rep],
            device_id={"replica": peer},
            device_id_type=MESH,
        )

    def g_copy(d):
        peer = (rep + d) % replicas
        return pltpu.make_async_remote_copy(
            src_ref=sync_out.at[rep],
            dst_ref=sync_out.at[rep],
            send_sem=g_send.at[d],
            recv_sem=g_recv.at[rep],
            device_id={"replica": peer},
            device_id_type=MESH,
        )

    far = [mask for mask in range(n // 2, n) if mask not in masks]
    near = [mask for mask in range(1, n // 2)]
    near_first = near[1:] + near[:1]
    waves = {"first": near, 0: masks + far}

    def x_wave(event):
        for mask in waves.get(event, []):
            x_copy(mask).start()

    for d in range(1, n):
        tok_copy(d).start()

    @pl.when(goes_right(0))
    def _():
        right(0).start()

    @pl.when(goes_left(0))
    def _():
        left(0).start()

    beside(chip, True).start()
    x_wave("first")

    loads[6].wait()

    def round_weight(i, carry):
        at = pl.ds(pl.multiple_of(i * 32, 32), 32)
        w_bf[at, :] = w_buf[at, :].astype(jnp.bfloat16)
        return carry

    lax.fori_loop(0, rows // 32, round_weight, 0)

    def send_term():
        for load in loads[:3]:
            load.wait()
        here = owner_ref[0] == rep
        slot = fragment_ref[0]

        for q in range(replicas):

            def term(i, carry, q=q):
                at = pl.ds(pl.multiple_of(q * quarter + i * step_rows, step_rows), step_rows)
                to = pl.ds(pl.multiple_of(i * step_rows, step_rows), step_rows)
                value = ((1.0 + outer_momentum) * outer_lr / replicas) * local_buf[slot, at, :]
                state = (1.0 - outer_lr * (1.0 + outer_momentum)) * global_buf[at, :] - (
                    outer_lr * outer_momentum * outer_momentum
                ) * mom_buf[at, :]
                value = value + jnp.where(here, state, 0.0)
                mine[q, to, :] = value.astype(jnp.bfloat16)
                return carry

            lax.fori_loop(0, quarter // step_rows, term, 0)
        for d in range(1, replicas):
            f_copy(d).start()

    def share_sums():
        for d in range(1, replicas):
            source = (rep + d) % replicas
            pltpu.make_async_remote_copy(
                src_ref=mine.at[source],
                dst_ref=parts.at[source],
                send_sem=f_send.at[d],
                recv_sem=f_recv.at[source],
                device_id={"replica": source},
                device_id_type=MESH,
            ).wait_recv()

        def add_parts(i, carry):
            to = pl.ds(pl.multiple_of(i * step_rows, step_rows), step_rows)
            total = mine[rep, to, :].astype(jnp.float32)
            for d in range(1, replicas):
                total = total + parts[(rep + d) % replicas, to, :].astype(jnp.float32)
            sync_out[rep, to, :] = total.astype(jnp.bfloat16)
            return carry

        lax.fori_loop(0, quarter // step_rows, add_parts, 0)
        for d in range(1, replicas):
            g_copy(d).start()

    send_term()
    for s in range(chips - 1):

        @pl.when(chip - 1 - s >= 0)
        def _(s=s):
            block = chip - 1 - s
            kc_copy(block_of(block), side, kc_send_side.at[0]).wait_recv()

            @pl.when(goes_right(s + 1))
            def _():
                right(s + 1).start()

            beside(block).start()

        @pl.when(chip + 1 + s < chips)
        def _(s=s):
            block = chip + 1 + s
            kc_copy(block_of(block), side, kc_send_side.at[0]).wait_recv()

            @pl.when(goes_left(s + 1))
            def _():
                left(s + 1).start()

            beside(block).start()

        x_wave(s)
        if s == min(1, chips - 2):
            share_sums()
            x_wave("shared")
    for load in loads[3:6]:
        load.wait()
    keep_cols = pltpu.make_async_copy(own_cols, cols_out.at[me], load_sem.at[0])
    keep_cols.start()

    for d in range(1, n):
        source = (me + d) % n
        pltpu.make_async_remote_copy(
            src_ref=tok_ref,
            dst_ref=tok_all.at[source],
            send_sem=tok_send.at[d],
            recv_sem=tok_recv.at[source],
            device_id={"fsdp": source},
            device_id_type=MESH,
        ).wait_recv()
    for j in range(chips):
        block = j * 2 + 1 - core
        kc_copy(block, side, kc_send_side.at[0]).wait_recv()

    half = HEAD // 2
    lane = lax.broadcasted_iota(jnp.int32, (tokens, HEAD), 1)
    sign = jnp.where(lane < half, 1.0, -1.0)
    exponent = (lax.broadcasted_iota(jnp.int32, (8, HEAD), 1) % half).astype(jnp.float32)
    frequency = jnp.exp(exponent * (-2.0 / HEAD * math.log(rope_base)))[0:1, :]
    row = lax.broadcasted_iota(jnp.int32, (tokens, tokens), 0)
    column = lax.broadcasted_iota(jnp.int32, (tokens, tokens), 1)

    def one_block(k):
        b = flip(me, k, n)

        def latest_of(j, latest):
            is_start = jnp.broadcast_to(tok_all[j], (tokens, tokens)) == begin_token
            at = j * tokens + column
            kept = jnp.where(
                jnp.logical_and(is_start, at <= b * tokens + row), at.astype(jnp.float32), -1.0
            )
            return jnp.maximum(latest, kept)

        latest = lax.fori_loop(0, n, latest_of, jnp.full((tokens, tokens), -1.0, jnp.float32))
        latest = jnp.max(latest, axis=1, keepdims=True)
        here_at = (b * tokens + lax.broadcasted_iota(jnp.int32, (tokens, HEAD), 0)).astype(
            jnp.float32
        )
        angles = (here_at - latest) * frequency
        cosine = jnp.cos(angles)
        sine = jnp.sin(angles) * sign
        for h in range(width // HEAD):
            at = slice(h * HEAD, (h + 1) * HEAD)
            value = kc_all[b, :, at].astype(jnp.float32)
            turned = value * cosine + pltpu.roll(value, half, 1) * sine
            kg_buf[b, :, at] = turned.astype(jnp.bfloat16)
        ic_buf[b] = lax.dot_general(
            kg_buf[b], w_bf[...], (((1,), (1,)), ((), ())), preferred_element_type=jnp.float32
        ).astype(jnp.bfloat16)

    def block_step(k, carry):
        mask = n - 1 - k
        one_block(mask)
        return carry

    lax.fori_loop(0, n, block_step, 0)
    for k in range(max(len(far), len(near))):
        for mask in far[k : k + 1] + near_first[k : k + 1]:
            ic_copy(mask).start()
    saves = [
        pltpu.make_async_copy(kg_buf, kg_out, save_sem.at[0]),
        pltpu.make_async_copy(ic_buf.at[me], ic_out.at[:, span_of(me)], save_sem.at[1]),
    ] + [
        pltpu.make_async_copy(ic_buf.at[flip(me, mask, n)], tail_out[k], save_sem.at[2 + k])
        for k, mask in enumerate(masks)
    ]
    for save in saves:
        save.start()

    for d in range(1, replicas):
        source = (rep + d) % replicas
        pltpu.make_async_remote_copy(
            src_ref=mine.at[source],
            dst_ref=sync_out.at[source],
            send_sem=g_send.at[d],
            recv_sem=g_recv.at[source],
            device_id={"replica": source},
            device_id_type=MESH,
        ).wait_recv()
        f_copy(d).wait_send()
        g_copy(d).wait_send()
    for d in range(1, n):
        tok_copy(d).wait_send()
    for s in range(chips - 1):

        @pl.when(goes_right(s))
        def _(s=s):
            right(s).wait_send()

        @pl.when(goes_left(s))
        def _(s=s):
            left(s).wait_send()

    for j in range(chips):
        beside(j).wait_send()
    keep_cols.wait()
    for save in saves:
        save.wait()
    for mask in range(1, n):
        x_copy(mask).wait_send()
        source = flip(me, mask, n)
        pltpu.make_async_remote_copy(
            src_ref=own_cols,
            dst_ref=cols_out.at[source],
            send_sem=x_send.at[mask],
            recv_sem=x_recv.at[source],
            device_id={"fsdp": source},
            device_id_type=MESH,
        ).wait_recv()
    for mask in far + near:
        ic_copy(mask).wait_send()
        source = flip(me, mask, n)
        pltpu.make_async_remote_copy(
            src_ref=ic_buf.at[source],
            dst_ref=ic_out.at[:, span_of(source)],
            send_sem=ic_send.at[mask],
            recv_sem=ic_recv.at[mask],
            device_id={"fsdp": source},
            device_id_type=MESH,
        ).wait_recv()


def on_device(
    token_ids,
    inputs,
    key_cotangent,
    key_weight,
    adam_m,
    adam_v,
    frag_local,
    frag_global,
    outer_mom,
    owner,
    fragment,
):
    tokens = inputs.shape[0]
    rows, width = key_weight.shape[1:]
    slots, _, frag_width = frag_local.shape[1:]
    n = lax.axis_size("fsdp")
    replicas = lax.axis_size("replica")
    seq_len = tokens * n
    quarter = rows // replicas
    tok = token_ids[None, :]
    anywhere = pl.BlockSpec(memory_space=pl.ANY)
    smem = pl.BlockSpec(memory_space=pltpu.SMEM)
    vmem = pl.BlockSpec(memory_space=pltpu.VMEM)
    hbm = pl.BlockSpec(memory_space=pltpu.HBM)
    dma = pltpu.SemaphoreType.DMA
    chips = n // 2
    bf16, f32 = jnp.bfloat16, jnp.float32
    masks = tail_masks(n)
    columns, key_grad, total, near_grad, *last = pl.pallas_call(
        functools.partial(exchange, n, replicas),
        out_shape=(
            jax.ShapeDtypeStruct((n, tokens, rows), bf16),
            jax.ShapeDtypeStruct((n, tokens, width), bf16),
            jax.ShapeDtypeStruct((replicas, quarter, frag_width), bf16),
            jax.ShapeDtypeStruct((tokens, n * rows), bf16),
        )
        + (jax.ShapeDtypeStruct((tokens, rows), bf16),) * len(masks),
        in_specs=[smem, smem, hbm, hbm] + [anywhere] * 5,
        out_specs=(anywhere, hbm, vmem, hbm) + (hbm,) * len(masks),
        scratch_shapes=[
            pltpu.VMEM((n, tokens, width), bf16),
            pltpu.VMEM((n, 1, tokens), jnp.int32),
            pltpu.VMEM((n, tokens, width), bf16),
            pltpu.VMEM((n, tokens, rows), bf16),
            pltpu.VMEM((rows, width), f32),
            pltpu.VMEM((rows, width), bf16),
            pltpu.VMEM((slots, rows, frag_width), f32),
            pltpu.VMEM((rows, frag_width), f32),
            pltpu.VMEM((rows, frag_width), f32),
            pltpu.VMEM((replicas, quarter, frag_width), bf16),
            pltpu.VMEM((replicas, quarter, frag_width), bf16),
            pltpu.VMEM((tokens, rows), bf16),
            dma((7,)),
            dma((2 + len(masks),)),
            dma((n,)),
            dma((n,)),
            dma((chips,)),
            dma((chips,)),
            dma((chips,)),
            dma((n,)),
            dma((n,)),
            dma((n,)),
            dma((n,)),
            dma((n,)),
            dma((replicas,)),
            dma((replicas,)),
            dma((replicas,)),
            dma((replicas,)),
        ],
        compiler_params=pltpu.CompilerParams(
            collective_id=0, has_side_effects=True, vmem_limit_bytes=63 * 1024 * 1024
        ),
    )(
        owner,
        fragment,
        tok,
        key_cotangent,
        inputs,
        key_weight[0],
        frag_local[0],
        frag_global[0],
        outer_mom[0],
    )
    last = [
        lax.ppermute(block, "fsdp", [(i, i ^ mask) for i in range(n)])
        for block, mask in zip(last, masks)
    ]
    size = tokens * n * rows * 2
    grad = jax.ShapeDtypeStruct((tokens, n * rows), bf16)
    input_cotangent = pl.pallas_call(
        functools.partial(through, n),
        out_shape=grad,
        in_specs=[anywhere],
        out_specs=anywhere,
        scratch_shapes=[pltpu.VMEM((tokens, n * rows), bf16), dma((n,)), dma((n,))],
        cost_estimate=pl.CostEstimate(flops=0, bytes_accessed=2 * size, transcendentals=0),
    )(near_grad)
    if masks:
        input_cotangent = pl.pallas_call(
            functools.partial(put_last, n),
            out_shape=grad,
            in_specs=[anywhere] + [vmem] * len(masks),
            out_specs=anywhere,
            scratch_shapes=[dma((len(masks),))],
            input_output_aliases={0: 0},
        )(input_cotangent, *last)
    weight_sum = lax.dot_general(
        columns.reshape(seq_len, rows),
        key_grad.reshape(seq_len, width),
        (((0,), (0,)), ((), ())),
        preferred_element_type=f32,
    )
    weight_grad = (weight_sum / seq_len)[None]
    moment_mean = beta_one * adam_m + (1.0 - beta_one) * weight_grad
    moment_square = beta_two * adam_v + (1.0 - beta_two) * weight_grad * weight_grad
    mean_hat = moment_mean / (1.0 - beta_one**adam_step)
    square_hat = moment_square / (1.0 - beta_two**adam_step)
    new_weight = key_weight - adam_lr * (
        mean_hat / (jnp.sqrt(square_hat) + adam_eps) + weight_decay * key_weight
    )
    is_owner = lax.axis_index("replica") == owner[0]
    synced = total.reshape(1, rows, frag_width).astype(f32)
    outer_grad = (
        frag_global - (outer_lr * outer_momentum * outer_momentum) * outer_mom - synced
    ) / (outer_lr * (1.0 + outer_momentum))
    new_outer_mom = jnp.where(is_owner, outer_momentum * outer_mom + outer_grad, outer_mom)
    return (input_cotangent, new_weight, moment_mean, moment_square, synced, new_outer_mom)


def solution(mesh):
    in_specs = (
        P(("replica", "fsdp")),
        P(("replica", "fsdp"), None),
        P(("replica", "fsdp"), None),
        P("replica", "fsdp", None),
        P("replica", "fsdp", None),
        P("replica", "fsdp", None),
        P("replica", None, "fsdp", None),
        P("replica", "fsdp", None),
        P("replica", "fsdp", None),
        P("fsdp"),
        P("replica"),
    )
    out_specs = (
        P(("replica", "fsdp"), None),
        P("replica", "fsdp", None),
        P("replica", "fsdp", None),
        P("replica", "fsdp", None),
        P("replica", "fsdp", None),
        P("replica", "fsdp", None),
    )
    return jax.shard_map(
        on_device, mesh=mesh, in_specs=in_specs, out_specs=out_specs, check_vma=False
    )
```

```python
import functools
import math

import jax
import jax.numpy as jnp
from jax import lax
from jax.experimental import pallas as pl
from jax.experimental.pallas import tpu as pltpu
from jax.sharding import PartitionSpec as P

HEAD = 128


begin_token = 128000
rope_base = 500000.0
beta_one = 0.9
beta_two = 0.95
adam_lr = 0.001
adam_eps = 1e-08
adam_step = 10.0
weight_decay = 0.1
outer_lr = 0.7
outer_momentum = 0.9


MESH = pl.DeviceIdType.MESH


def flip(index, mask, size):
    total, bit = 0, 1
    while bit < size:
        own, other = (index // bit) % 2, (mask // bit) % 2
        total = total + bit * (own + other - 2 * own * other)
        bit *= 2
    return total


def tail_masks(n):
    return [mask for mask in (n // 2, n // 2 + n // 4) if mask % 2 == 0] if n > 4 else []


def through(n, blocks_ref, out_ref, held, in_sem, out_sem):
    rows = blocks_ref.shape[1] // n
    spans = [slice(j * rows, (j + 1) * rows) for j in range(n)]
    arrive = [
        pltpu.make_async_copy(blocks_ref.at[:, at], held.at[:, at], in_sem.at[j])
        for j, at in enumerate(spans)
    ]
    leave = [
        pltpu.make_async_copy(held.at[:, at], out_ref.at[:, at], out_sem.at[j])
        for j, at in enumerate(spans)
    ]
    for copy in arrive:
        copy.start()
    for j in range(n):
        arrive[j].wait()
        leave[j].start()
    for copy in leave:
        copy.wait()


def put_last(n, *refs):
    masks = tail_masks(n)
    blocks, out_ref, sem = refs[1 : 1 + len(masks)], refs[-2], refs[-1]
    me = lax.axis_index("fsdp")
    rows = blocks[0].shape[1]
    copies = []
    for k, mask in enumerate(masks):
        at = pl.ds(pl.multiple_of(flip(me, mask, n) * rows, rows), rows)
        copies.append(pltpu.make_async_copy(blocks[k], out_ref.at[:, at], sem.at[k]))
    for copy in copies:
        copy.start()
    for copy in copies:
        copy.wait()


def exchange(
    n,
    replicas,
    owner_ref,
    fragment_ref,
    tok_ref,
    kc_hbm,
    x_hbm,
    w_hbm,
    local_hbm,
    global_hbm,
    mom_hbm,
    *rest,
):
    masks = tail_masks(n)
    cols_out, kg_out, sync_out, ic_out = rest[:4]
    tail_out, rest = rest[4 : 4 + len(masks)], rest[4 + len(masks) :]
    (
        kc_all,
        tok_all,
        kg_buf,
        ic_buf,
        w_buf,
        w_bf,
        local_buf,
        global_buf,
        mom_buf,
        mine,
        parts,
        own_cols,
        load_sem,
        save_sem,
        tok_send,
        tok_recv,
        kc_send_right,
        kc_send_left,
        kc_send_side,
        kc_recv,
        x_send,
        x_recv,
        ic_send,
        ic_recv,
        f_send,
        f_recv,
        g_send,
        g_recv,
    ) = rest
    me = lax.axis_index("fsdp")
    rep = lax.axis_index("replica")
    chips = n // 2
    chip, core = me // 2, me % 2
    side = me + 1 - 2 * core
    tokens, width = kc_hbm.shape
    rows = w_hbm.shape[0]
    quarter = rows // replicas
    step_rows = min(32, quarter)

    barrier = pltpu.get_barrier_semaphore()
    for d in range(1, n):
        pl.semaphore_signal(
            barrier, inc=1, device_id={"fsdp": (me + d) % n}, device_id_type=MESH
        )
    for d in range(1, replicas):
        pl.semaphore_signal(
            barrier, inc=1, device_id={"replica": (rep + d) % replicas}, device_id_type=MESH
        )

    loads = [
        pltpu.make_async_copy(local_hbm, local_buf, load_sem.at[0]),
        pltpu.make_async_copy(global_hbm, global_buf, load_sem.at[1]),
        pltpu.make_async_copy(mom_hbm, mom_buf, load_sem.at[2]),
        pltpu.make_async_copy(kc_hbm, kc_all.at[me], load_sem.at[3]),
        pltpu.make_async_copy(tok_ref, tok_all.at[me], load_sem.at[4]),
        pltpu.make_async_copy(
            x_hbm.at[:, pl.ds(pl.multiple_of(me * rows, rows), rows)], own_cols, load_sem.at[5]
        ),
        pltpu.make_async_copy(w_hbm, w_buf, load_sem.at[6]),
    ]
    for load in loads:
        load.start()
    pl.semaphore_wait(barrier, n - 1 + replicas - 1)

    def tok_copy(d):
        return pltpu.make_async_remote_copy(
            src_ref=tok_ref,
            dst_ref=tok_all.at[me],
            send_sem=tok_send.at[d],
            recv_sem=tok_recv.at[me],
            device_id={"fsdp": (me + d) % n},
            device_id_type=MESH,
        )

    def kc_copy(block, target, send_sem, first=False):
        return pltpu.make_async_remote_copy(
            src_ref=kc_hbm if first else kc_all.at[block],
            dst_ref=kc_all.at[block],
            send_sem=send_sem,
            recv_sem=kc_recv.at[block],
            device_id={"fsdp": target},
            device_id_type=MESH,
        )

    def block_of(at_chip):
        return jnp.clip(at_chip, 0, chips - 1) * 2 + core

    def right(s):
        target = jnp.minimum(me + 2, n - 1)
        return kc_copy(block_of(chip - s), target, kc_send_right.at[s], s == 0)

    def left(s):
        target = jnp.maximum(me - 2, 0)
        return kc_copy(block_of(chip + s), target, kc_send_left.at[s], s == 0)

    def goes_right(s):
        return jnp.logical_and(chip - s >= 0, chip + 1 < chips)

    def goes_left(s):
        return jnp.logical_and(chip + s < chips, chip >= 1)

    def beside(at_chip, first=False):
        at = jnp.clip(at_chip, 0, chips - 1)
        return kc_copy(at * 2 + core, side, kc_send_side.at[at], first)

    def x_copy(mask):
        peer = flip(me, mask, n)
        return pltpu.make_async_remote_copy(
            src_ref=x_hbm.at[:, pl.ds(pl.multiple_of(peer * rows, rows), rows)],
            dst_ref=cols_out.at[me],
            send_sem=x_send.at[mask],
            recv_sem=x_recv.at[me],
            device_id={"fsdp": peer},
            device_id_type=MESH,
        )

    def span_of(at):
        return pl.ds(pl.multiple_of(at * rows, rows), rows)

    def ic_copy(mask):
        peer = flip(me, mask, n)
        return pltpu.make_async_remote_copy(
            src_ref=ic_buf.at[peer],
            dst_ref=ic_out.at[:, span_of(me)],
            send_sem=ic_send.at[mask],
            recv_sem=ic_recv.at[mask],
            device_id={"fsdp": peer},
            device_id_type=MESH,
        )

    def f_copy(d):
        peer = (rep + d) % replicas
        return pltpu.make_async_remote_copy(
            src_ref=mine.at[peer],
            dst_ref=parts.at[rep],
            send_sem=f_send.at[d],
            recv_sem=f_recv.at[rep],
            device_id={"replica": peer},
            device_id_type=MESH,
        )

    def g_copy(d):
        peer = (rep + d) % replicas
        return pltpu.make_async_remote_copy(
            src_ref=sync_out.at[rep],
            dst_ref=sync_out.at[rep],
            send_sem=g_send.at[d],
            recv_sem=g_recv.at[rep],
            device_id={"replica": peer},
            device_id_type=MESH,
        )

    far = [mask for mask in range(n // 2, n) if mask not in masks]
    near = [mask for mask in range(1, n // 2)]
    near_first = near[1:] + near[:1]
    waves = {"first": near + far[-1:], 0: masks[::-1] + far[:-1]}

    def x_wave(event):
        for mask in waves.get(event, []):
            x_copy(mask).start()

    for d in range(1, n):
        tok_copy(d).start()

    @pl.when(goes_right(0))
    def _():
        right(0).start()

    @pl.when(goes_left(0))
    def _():
        left(0).start()

    beside(chip, True).start()
    x_wave("first")

    loads[6].wait()

    def round_weight(i, carry):
        at = pl.ds(pl.multiple_of(i * 32, 32), 32)
        w_bf[at, :] = w_buf[at, :].astype(jnp.bfloat16)
        return carry

    lax.fori_loop(0, rows // 32, round_weight, 0)

    def send_term():
        for load in loads[:3]:
            load.wait()
        here = owner_ref[0] == rep
        slot = fragment_ref[0]

        for q in range(replicas):

            def term(i, carry, q=q):
                at = pl.ds(pl.multiple_of(q * quarter + i * step_rows, step_rows), step_rows)
                to = pl.ds(pl.multiple_of(i * step_rows, step_rows), step_rows)
                value = ((1.0 + outer_momentum) * outer_lr / replicas) * local_buf[slot, at, :]
                state = (1.0 - outer_lr * (1.0 + outer_momentum)) * global_buf[at, :] - (
                    outer_lr * outer_momentum * outer_momentum
                ) * mom_buf[at, :]
                value = value + jnp.where(here, state, 0.0)
                mine[q, to, :] = value.astype(jnp.bfloat16)
                return carry

            lax.fori_loop(0, quarter // step_rows, term, 0)
        for d in range(1, replicas):
            f_copy(d).start()

    def share_sums():
        for d in range(1, replicas):
            source = (rep + d) % replicas
            pltpu.make_async_remote_copy(
                src_ref=mine.at[source],
                dst_ref=parts.at[source],
                send_sem=f_send.at[d],
                recv_sem=f_recv.at[source],
                device_id={"replica": source},
                device_id_type=MESH,
            ).wait_recv()

        def add_parts(i, carry):
            to = pl.ds(pl.multiple_of(i * step_rows, step_rows), step_rows)
            total = mine[rep, to, :].astype(jnp.float32)
            for d in range(1, replicas):
                total = total + parts[(rep + d) % replicas, to, :].astype(jnp.float32)
            sync_out[rep, to, :] = total.astype(jnp.bfloat16)
            return carry

        lax.fori_loop(0, quarter // step_rows, add_parts, 0)
        for d in range(1, replicas):
            g_copy(d).start()

    for s in range(chips - 1):

        @pl.when(chip - 1 - s >= 0)
        def _(s=s):
            block = chip - 1 - s
            kc_copy(block_of(block), side, kc_send_side.at[0]).wait_recv()

            @pl.when(goes_right(s + 1))
            def _():
                right(s + 1).start()

            beside(block).start()

        @pl.when(chip + 1 + s < chips)
        def _(s=s):
            block = chip + 1 + s
            kc_copy(block_of(block), side, kc_send_side.at[0]).wait_recv()

            @pl.when(goes_left(s + 1))
            def _():
                left(s + 1).start()

            beside(block).start()

        x_wave(s)
        if s == 0:
            send_term()
        if s == min(1, chips - 2):
            share_sums()
    for load in loads[3:6]:
        load.wait()
    keep_cols = pltpu.make_async_copy(own_cols, cols_out.at[me], load_sem.at[0])
    keep_cols.start()

    for d in range(1, n):
        source = (me + d) % n
        pltpu.make_async_remote_copy(
            src_ref=tok_ref,
            dst_ref=tok_all.at[source],
            send_sem=tok_send.at[d],
            recv_sem=tok_recv.at[source],
            device_id={"fsdp": source},
            device_id_type=MESH,
        ).wait_recv()
    for j in range(chips):
        block = j * 2 + 1 - core
        kc_copy(block, side, kc_send_side.at[0]).wait_recv()

    half = HEAD // 2
    lane = lax.broadcasted_iota(jnp.int32, (tokens, HEAD), 1)
    sign = jnp.where(lane < half, 1.0, -1.0)
    exponent = (lax.broadcasted_iota(jnp.int32, (8, HEAD), 1) % half).astype(jnp.float32)
    frequency = jnp.exp(exponent * (-2.0 / HEAD * math.log(rope_base)))[0:1, :]
    row = lax.broadcasted_iota(jnp.int32, (tokens, tokens), 0)
    column = lax.broadcasted_iota(jnp.int32, (tokens, tokens), 1)

    def one_block(k):
        b = flip(me, k, n)

        def latest_of(j, latest):
            is_start = jnp.broadcast_to(tok_all[j], (tokens, tokens)) == begin_token
            at = j * tokens + column
            kept = jnp.where(
                jnp.logical_and(is_start, at <= b * tokens + row), at.astype(jnp.float32), -1.0
            )
            return jnp.maximum(latest, kept)

        latest = lax.fori_loop(0, n, latest_of, jnp.full((tokens, tokens), -1.0, jnp.float32))
        latest = jnp.max(latest, axis=1, keepdims=True)
        here_at = (b * tokens + lax.broadcasted_iota(jnp.int32, (tokens, HEAD), 0)).astype(
            jnp.float32
        )
        angles = (here_at - latest) * frequency
        cosine = jnp.cos(angles)
        sine = jnp.sin(angles) * sign
        for h in range(width // HEAD):
            at = slice(h * HEAD, (h + 1) * HEAD)
            value = kc_all[b, :, at].astype(jnp.float32)
            turned = value * cosine + pltpu.roll(value, half, 1) * sine
            kg_buf[b, :, at] = turned.astype(jnp.bfloat16)
        ic_buf[b] = lax.dot_general(
            kg_buf[b], w_bf[...], (((1,), (1,)), ((), ())), preferred_element_type=jnp.float32
        ).astype(jnp.bfloat16)

    def block_step(k, carry):
        mask = n - 1 - k
        one_block(mask)
        return carry

    lax.fori_loop(0, n, block_step, 0)
    for k in range(max(len(far), len(near))):
        for mask in far[k : k + 1] + near_first[k : k + 1]:
            ic_copy(mask).start()
    saves = [
        pltpu.make_async_copy(kg_buf, kg_out, save_sem.at[0]),
        pltpu.make_async_copy(ic_buf.at[me], ic_out.at[:, span_of(me)], save_sem.at[1]),
    ] + [
        pltpu.make_async_copy(ic_buf.at[flip(me, mask, n)], tail_out[k], save_sem.at[2 + k])
        for k, mask in enumerate(masks)
    ]
    for save in saves:
        save.start()

    for d in range(1, replicas):
        source = (rep + d) % replicas
        pltpu.make_async_remote_copy(
            src_ref=mine.at[source],
            dst_ref=sync_out.at[source],
            send_sem=g_send.at[d],
            recv_sem=g_recv.at[source],
            device_id={"replica": source},
            device_id_type=MESH,
        ).wait_recv()
        f_copy(d).wait_send()
        g_copy(d).wait_send()
    for d in range(1, n):
        tok_copy(d).wait_send()
    for s in range(chips - 1):

        @pl.when(goes_right(s))
        def _(s=s):
            right(s).wait_send()

        @pl.when(goes_left(s))
        def _(s=s):
            left(s).wait_send()

    for j in range(chips):
        beside(j).wait_send()
    keep_cols.wait()
    for save in saves:
        save.wait()
    for mask in range(1, n):
        x_copy(mask).wait_send()
        source = flip(me, mask, n)
        pltpu.make_async_remote_copy(
            src_ref=own_cols,
            dst_ref=cols_out.at[source],
            send_sem=x_send.at[mask],
            recv_sem=x_recv.at[source],
            device_id={"fsdp": source},
            device_id_type=MESH,
        ).wait_recv()
    for mask in far + near:
        ic_copy(mask).wait_send()
        source = flip(me, mask, n)
        pltpu.make_async_remote_copy(
            src_ref=ic_buf.at[source],
            dst_ref=ic_out.at[:, span_of(source)],
            send_sem=ic_send.at[mask],
            recv_sem=ic_recv.at[mask],
            device_id={"fsdp": source},
            device_id_type=MESH,
        ).wait_recv()


def on_device(
    token_ids,
    inputs,
    key_cotangent,
    key_weight,
    adam_m,
    adam_v,
    frag_local,
    frag_global,
    outer_mom,
    owner,
    fragment,
):
    tokens = inputs.shape[0]
    rows, width = key_weight.shape[1:]
    slots, _, frag_width = frag_local.shape[1:]
    n = lax.axis_size("fsdp")
    replicas = lax.axis_size("replica")
    seq_len = tokens * n
    quarter = rows // replicas
    tok = token_ids[None, :]
    anywhere = pl.BlockSpec(memory_space=pl.ANY)
    smem = pl.BlockSpec(memory_space=pltpu.SMEM)
    vmem = pl.BlockSpec(memory_space=pltpu.VMEM)
    hbm = pl.BlockSpec(memory_space=pltpu.HBM)
    dma = pltpu.SemaphoreType.DMA
    chips = n // 2
    bf16, f32 = jnp.bfloat16, jnp.float32
    masks = tail_masks(n)
    columns, key_grad, total, near_grad, *last = pl.pallas_call(
        functools.partial(exchange, n, replicas),
        out_shape=(
            jax.ShapeDtypeStruct((n, tokens, rows), bf16),
            jax.ShapeDtypeStruct((n, tokens, width), bf16),
            jax.ShapeDtypeStruct((replicas, quarter, frag_width), bf16),
            jax.ShapeDtypeStruct((tokens, n * rows), bf16),
        )
        + (jax.ShapeDtypeStruct((tokens, rows), bf16),) * len(masks),
        in_specs=[smem, smem, hbm, hbm] + [anywhere] * 5,
        out_specs=(anywhere, hbm, vmem, hbm) + (hbm,) * len(masks),
        scratch_shapes=[
            pltpu.VMEM((n, tokens, width), bf16),
            pltpu.VMEM((n, 1, tokens), jnp.int32),
            pltpu.VMEM((n, tokens, width), bf16),
            pltpu.VMEM((n, tokens, rows), bf16),
            pltpu.VMEM((rows, width), f32),
            pltpu.VMEM((rows, width), bf16),
            pltpu.VMEM((slots, rows, frag_width), f32),
            pltpu.VMEM((rows, frag_width), f32),
            pltpu.VMEM((rows, frag_width), f32),
            pltpu.VMEM((replicas, quarter, frag_width), bf16),
            pltpu.VMEM((replicas, quarter, frag_width), bf16),
            pltpu.VMEM((tokens, rows), bf16),
            dma((7,)),
            dma((2 + len(masks),)),
            dma((n,)),
            dma((n,)),
            dma((chips,)),
            dma((chips,)),
            dma((chips,)),
            dma((n,)),
            dma((n,)),
            dma((n,)),
            dma((n,)),
            dma((n,)),
            dma((replicas,)),
            dma((replicas,)),
            dma((replicas,)),
            dma((replicas,)),
        ],
        compiler_params=pltpu.CompilerParams(
            collective_id=0, has_side_effects=True, vmem_limit_bytes=63 * 1024 * 1024
        ),
    )(
        owner,
        fragment,
        tok,
        key_cotangent,
        inputs,
        key_weight[0],
        frag_local[0],
        frag_global[0],
        outer_mom[0],
    )
    last = [
        lax.ppermute(block, "fsdp", [(i, i ^ mask) for i in range(n)])
        for block, mask in zip(last, masks)
    ]
    size = tokens * n * rows * 2
    grad = jax.ShapeDtypeStruct((tokens, n * rows), bf16)
    input_cotangent = pl.pallas_call(
        functools.partial(through, n),
        out_shape=grad,
        in_specs=[anywhere],
        out_specs=anywhere,
        scratch_shapes=[pltpu.VMEM((tokens, n * rows), bf16), dma((n,)), dma((n,))],
        cost_estimate=pl.CostEstimate(flops=0, bytes_accessed=2 * size, transcendentals=0),
    )(near_grad)
    if masks:
        input_cotangent = pl.pallas_call(
            functools.partial(put_last, n),
            out_shape=grad,
            in_specs=[anywhere] * (1 + len(masks)),
            out_specs=anywhere,
            scratch_shapes=[dma((len(masks),))],
            input_output_aliases={0: 0},
        )(input_cotangent, *[pltpu.with_memory_space_constraint(block, pltpu.VMEM) for block in last])
    weight_sum = lax.dot_general(
        columns.reshape(seq_len, rows),
        key_grad.reshape(seq_len, width),
        (((0,), (0,)), ((), ())),
        preferred_element_type=f32,
    )
    weight_grad = (weight_sum / seq_len)[None]
    moment_mean = beta_one * adam_m + (1.0 - beta_one) * weight_grad
    moment_square = beta_two * adam_v + (1.0 - beta_two) * weight_grad * weight_grad
    mean_hat = moment_mean / (1.0 - beta_one**adam_step)
    square_hat = moment_square / (1.0 - beta_two**adam_step)
    new_weight = key_weight - adam_lr * (
        mean_hat / (jnp.sqrt(square_hat) + adam_eps) + weight_decay * key_weight
    )
    is_owner = lax.axis_index("replica") == owner[0]
    synced = total.reshape(1, rows, frag_width).astype(f32)
    outer_grad = (
        frag_global - (outer_lr * outer_momentum * outer_momentum) * outer_mom - synced
    ) / (outer_lr * (1.0 + outer_momentum))
    new_outer_mom = jnp.where(is_owner, outer_momentum * outer_mom + outer_grad, outer_mom)
    return (input_cotangent, new_weight, moment_mean, moment_square, synced, new_outer_mom)


def solution(mesh):
    in_specs = (
        P(("replica", "fsdp")),
        P(("replica", "fsdp"), None),
        P(("replica", "fsdp"), None),
        P("replica", "fsdp", None),
        P("replica", "fsdp", None),
        P("replica", "fsdp", None),
        P("replica", None, "fsdp", None),
        P("replica", "fsdp", None),
        P("replica", "fsdp", None),
        P("fsdp"),
        P("replica"),
    )
    out_specs = (
        P(("replica", "fsdp"), None),
        P("replica", "fsdp", None),
        P("replica", "fsdp", None),
        P("replica", "fsdp", None),
        P("replica", "fsdp", None),
        P("replica", "fsdp", None),
    )
    return jax.shard_map(
        on_device, mesh=mesh, in_specs=in_specs, out_specs=out_specs, check_vma=False
    )
```

```python
import functools
import math

import jax
import jax.numpy as jnp
from jax import lax
from jax.experimental import pallas as pl
from jax.experimental.pallas import tpu as pltpu
from jax.sharding import PartitionSpec as P

HEAD = 128


begin_token = 128000
rope_base = 500000.0
beta_one = 0.9
beta_two = 0.95
adam_lr = 0.001
adam_eps = 1e-08
adam_step = 10.0
weight_decay = 0.1
outer_lr = 0.7
outer_momentum = 0.9


MESH = pl.DeviceIdType.MESH


def flip(index, mask, size):
    total, bit = 0, 1
    while bit < size:
        own, other = (index // bit) % 2, (mask // bit) % 2
        total = total + bit * (own + other - 2 * own * other)
        bit *= 2
    return total


def tail_masks(n):
    return [n // 2 + 1, n - 1] if n > 4 else []


def through(n, blocks_ref, out_ref, held, in_sem, out_sem):
    rows = blocks_ref.shape[1] // n
    spans = [slice(j * rows, (j + 1) * rows) for j in range(n)]
    arrive = [
        pltpu.make_async_copy(blocks_ref.at[:, at], held.at[:, at], in_sem.at[j])
        for j, at in enumerate(spans)
    ]
    leave = [
        pltpu.make_async_copy(held.at[:, at], out_ref.at[:, at], out_sem.at[j])
        for j, at in enumerate(spans)
    ]
    for copy in arrive:
        copy.start()
    for j in range(n):
        arrive[j].wait()
        leave[j].start()
    for copy in leave:
        copy.wait()


def put_last(n, *refs):
    masks = tail_masks(n)
    blocks, out_ref, sem = refs[1 : 1 + len(masks)], refs[-2], refs[-1]
    me = lax.axis_index("fsdp")
    rows = blocks[0].shape[1]
    copies = []
    for k, mask in enumerate(masks):
        at = pl.ds(pl.multiple_of(flip(me, mask, n) * rows, rows), rows)
        copies.append(pltpu.make_async_copy(blocks[k], out_ref.at[:, at], sem.at[k]))
    for copy in copies:
        copy.start()
    for copy in copies:
        copy.wait()


def exchange(
    n,
    replicas,
    owner_ref,
    fragment_ref,
    tok_ref,
    kc_hbm,
    x_hbm,
    w_hbm,
    local_hbm,
    global_hbm,
    mom_hbm,
    *rest,
):
    masks = tail_masks(n)
    cols_out, kg_out, sync_out, ic_out = rest[:4]
    tail_out, rest = rest[4 : 4 + len(masks)], rest[4 + len(masks) :]
    (
        kc_all,
        tok_all,
        kg_buf,
        ic_buf,
        w_buf,
        w_bf,
        local_buf,
        global_buf,
        mom_buf,
        mine,
        parts,
        own_cols,
        load_sem,
        save_sem,
        tok_send,
        tok_recv,
        kc_send_right,
        kc_send_left,
        kc_send_side,
        kc_recv,
        x_send,
        x_recv,
        ic_send,
        ic_recv,
        f_send,
        f_recv,
        g_send,
        g_recv,
    ) = rest
    me = lax.axis_index("fsdp")
    rep = lax.axis_index("replica")
    chips = n // 2
    chip, core = me // 2, me % 2
    side = me + 1 - 2 * core
    tokens, width = kc_hbm.shape
    rows = w_hbm.shape[0]
    quarter = rows // replicas
    step_rows = min(32, quarter)

    barrier = pltpu.get_barrier_semaphore()
    for d in range(1, n):
        pl.semaphore_signal(
            barrier, inc=1, device_id={"fsdp": (me + d) % n}, device_id_type=MESH
        )
    for d in range(1, replicas):
        pl.semaphore_signal(
            barrier, inc=1, device_id={"replica": (rep + d) % replicas}, device_id_type=MESH
        )

    loads = [
        pltpu.make_async_copy(local_hbm, local_buf, load_sem.at[0]),
        pltpu.make_async_copy(global_hbm, global_buf, load_sem.at[1]),
        pltpu.make_async_copy(mom_hbm, mom_buf, load_sem.at[2]),
        pltpu.make_async_copy(kc_hbm, kc_all.at[me], load_sem.at[3]),
        pltpu.make_async_copy(tok_ref, tok_all.at[me], load_sem.at[4]),
        pltpu.make_async_copy(
            x_hbm.at[:, pl.ds(pl.multiple_of(me * rows, rows), rows)], own_cols, load_sem.at[5]
        ),
        pltpu.make_async_copy(w_hbm, w_buf, load_sem.at[6]),
    ]
    for load in loads:
        load.start()
    pl.semaphore_wait(barrier, n - 1 + replicas - 1)

    def tok_copy(d):
        return pltpu.make_async_remote_copy(
            src_ref=tok_ref,
            dst_ref=tok_all.at[me],
            send_sem=tok_send.at[d],
            recv_sem=tok_recv.at[me],
            device_id={"fsdp": (me + d) % n},
            device_id_type=MESH,
        )

    def kc_copy(block, target, send_sem, first=False):
        return pltpu.make_async_remote_copy(
            src_ref=kc_hbm if first else kc_all.at[block],
            dst_ref=kc_all.at[block],
            send_sem=send_sem,
            recv_sem=kc_recv.at[block],
            device_id={"fsdp": target},
            device_id_type=MESH,
        )

    def block_of(at_chip):
        return jnp.clip(at_chip, 0, chips - 1) * 2 + core

    def right(s):
        target = jnp.minimum(me + 2, n - 1)
        return kc_copy(block_of(chip - s), target, kc_send_right.at[s], s == 0)

    def left(s):
        target = jnp.maximum(me - 2, 0)
        return kc_copy(block_of(chip + s), target, kc_send_left.at[s], s == 0)

    def goes_right(s):
        return jnp.logical_and(chip - s >= 0, chip + 1 < chips)

    def goes_left(s):
        return jnp.logical_and(chip + s < chips, chip >= 1)

    def beside(at_chip, first=False):
        at = jnp.clip(at_chip, 0, chips - 1)
        return kc_copy(at * 2 + core, side, kc_send_side.at[at], first)

    def x_copy(mask):
        peer = flip(me, mask, n)
        return pltpu.make_async_remote_copy(
            src_ref=x_hbm.at[:, pl.ds(pl.multiple_of(peer * rows, rows), rows)],
            dst_ref=cols_out.at[me],
            send_sem=x_send.at[mask],
            recv_sem=x_recv.at[me],
            device_id={"fsdp": peer},
            device_id_type=MESH,
        )

    def span_of(at):
        return pl.ds(pl.multiple_of(at * rows, rows), rows)

    def ic_copy(mask):
        peer = flip(me, mask, n)
        return pltpu.make_async_remote_copy(
            src_ref=ic_buf.at[peer],
            dst_ref=ic_out.at[:, span_of(me)],
            send_sem=ic_send.at[mask],
            recv_sem=ic_recv.at[mask],
            device_id={"fsdp": peer},
            device_id_type=MESH,
        )

    def f_copy(d):
        peer = (rep + d) % replicas
        return pltpu.make_async_remote_copy(
            src_ref=mine.at[peer],
            dst_ref=parts.at[rep],
            send_sem=f_send.at[d],
            recv_sem=f_recv.at[rep],
            device_id={"replica": peer},
            device_id_type=MESH,
        )

    def g_copy(d):
        peer = (rep + d) % replicas
        return pltpu.make_async_remote_copy(
            src_ref=sync_out.at[rep],
            dst_ref=sync_out.at[rep],
            send_sem=g_send.at[d],
            recv_sem=g_recv.at[rep],
            device_id={"replica": peer},
            device_id_type=MESH,
        )

    far = [mask for mask in range(n // 2, n) if mask not in masks]
    near = [mask for mask in range(1, n // 2)]
    near_first = near[1:] + near[:1]
    waves = {"first": near + far[-1:], 0: masks[::-1] + far[:-1]}

    def x_wave(event):
        for mask in waves.get(event, []):
            x_copy(mask).start()

    @pl.when(goes_right(0))
    def _():
        right(0).start()

    @pl.when(goes_left(0))
    def _():
        left(0).start()

    beside(chip, True).start()
    x_wave("first")
    for d in range(1, n):
        tok_copy(d).start()

    loads[6].wait()

    def round_weight(i, carry):
        at = pl.ds(pl.multiple_of(i * 32, 32), 32)
        w_bf[at, :] = w_buf[at, :].astype(jnp.bfloat16)
        return carry

    lax.fori_loop(0, rows // 32, round_weight, 0)

    def send_term():
        for load in loads[:3]:
            load.wait()
        here = owner_ref[0] == rep
        slot = fragment_ref[0]

        for q in range(replicas):

            def term(i, carry, q=q):
                at = pl.ds(pl.multiple_of(q * quarter + i * step_rows, step_rows), step_rows)
                to = pl.ds(pl.multiple_of(i * step_rows, step_rows), step_rows)
                value = ((1.0 + outer_momentum) * outer_lr / replicas) * local_buf[slot, at, :]
                state = (1.0 - outer_lr * (1.0 + outer_momentum)) * global_buf[at, :] - (
                    outer_lr * outer_momentum * outer_momentum
                ) * mom_buf[at, :]
                value = value + jnp.where(here, state, 0.0)
                mine[q, to, :] = value.astype(jnp.bfloat16)
                return carry

            lax.fori_loop(0, quarter // step_rows, term, 0)
        for d in range(1, replicas):
            f_copy(d).start()

    def share_sums():
        for d in range(1, replicas):
            source = (rep + d) % replicas
            pltpu.make_async_remote_copy(
                src_ref=mine.at[source],
                dst_ref=parts.at[source],
                send_sem=f_send.at[d],
                recv_sem=f_recv.at[source],
                device_id={"replica": source},
                device_id_type=MESH,
            ).wait_recv()

        def add_parts(i, carry):
            to = pl.ds(pl.multiple_of(i * step_rows, step_rows), step_rows)
            total = mine[rep, to, :].astype(jnp.float32)
            for d in range(1, replicas):
                total = total + parts[(rep + d) % replicas, to, :].astype(jnp.float32)
            sync_out[rep, to, :] = total.astype(jnp.bfloat16)
            return carry

        lax.fori_loop(0, quarter // step_rows, add_parts, 0)
        for d in range(1, replicas):
            g_copy(d).start()

    half = HEAD // 2
    lane = lax.broadcasted_iota(jnp.int32, (tokens, HEAD), 1)
    sign = jnp.where(lane < half, 1.0, -1.0)
    exponent = (lax.broadcasted_iota(jnp.int32, (8, HEAD), 1) % half).astype(jnp.float32)
    frequency = jnp.exp(exponent * (-2.0 / HEAD * math.log(rope_base)))[0:1, :]
    row = lax.broadcasted_iota(jnp.int32, (tokens, tokens), 0)
    column = lax.broadcasted_iota(jnp.int32, (tokens, tokens), 1)

    def one_block(k):
        b = flip(me, k, n)

        def latest_of(j, latest):
            is_start = jnp.broadcast_to(tok_all[j], (tokens, tokens)) == begin_token
            at = j * tokens + column
            kept = jnp.where(
                jnp.logical_and(is_start, at <= b * tokens + row), at.astype(jnp.float32), -1.0
            )
            return jnp.maximum(latest, kept)

        latest = lax.fori_loop(0, n, latest_of, jnp.full((tokens, tokens), -1.0, jnp.float32))
        latest = jnp.max(latest, axis=1, keepdims=True)
        here_at = (b * tokens + lax.broadcasted_iota(jnp.int32, (tokens, HEAD), 0)).astype(
            jnp.float32
        )
        angles = (here_at - latest) * frequency
        cosine = jnp.cos(angles)
        sine = jnp.sin(angles) * sign
        for h in range(width // HEAD):
            at = slice(h * HEAD, (h + 1) * HEAD)
            value = kc_all[b, :, at].astype(jnp.float32)
            turned = value * cosine + pltpu.roll(value, half, 1) * sine
            kg_buf[b, :, at] = turned.astype(jnp.bfloat16)
        ic_buf[b] = lax.dot_general(
            kg_buf[b], w_bf[...], (((1,), (1,)), ((), ())), preferred_element_type=jnp.float32
        ).astype(jnp.bfloat16)

    def block_step(k, carry):
        @pl.when(k % 2 == 1)
        def _():
            kc_copy(flip(me, k, n), side, kc_send_side.at[0]).wait_recv()

        one_block(k)
        sent = k > 0
        for last in masks:
            sent = jnp.logical_and(sent, k != last)

        @pl.when(sent)
        def _():
            ic_copy(k).start()

        return carry

    def near_blocks():
        for load in loads[3:5]:
            load.wait()
        for d in range(1, n):
            source = (me + d) % n
            pltpu.make_async_remote_copy(
                src_ref=tok_ref,
                dst_ref=tok_all.at[source],
                send_sem=tok_send.at[d],
                recv_sem=tok_recv.at[source],
                device_id={"fsdp": source},
                device_id_type=MESH,
            ).wait_recv()
        lax.fori_loop(0, n // 2, block_step, 0)

    def far_step(j, carry):
        k = n // 2 + 2 * (j % (n // 4)) + j // (n // 4)
        return block_step(k, carry)

    for s in range(chips - 1):
        if s == chips - 2:
            near_blocks()

        @pl.when(chip - 1 - s >= 0)
        def _(s=s):
            block = chip - 1 - s
            kc_copy(block_of(block), side, kc_send_side.at[0]).wait_recv()

            @pl.when(goes_right(s + 1))
            def _():
                right(s + 1).start()

            beside(block).start()

        @pl.when(chip + 1 + s < chips)
        def _(s=s):
            block = chip + 1 + s
            kc_copy(block_of(block), side, kc_send_side.at[0]).wait_recv()

            @pl.when(goes_left(s + 1))
            def _():
                left(s + 1).start()

            beside(block).start()

        x_wave(s)
        if s == 0:
            send_term()
        if s == min(1, chips - 2):
            share_sums()
    lax.fori_loop(0, n // 2, far_step, 0)
    loads[5].wait()
    keep_cols = pltpu.make_async_copy(own_cols, cols_out.at[me], load_sem.at[0])
    keep_cols.start()

    saves = [
        pltpu.make_async_copy(kg_buf, kg_out, save_sem.at[0]),
        pltpu.make_async_copy(ic_buf.at[me], ic_out.at[:, span_of(me)], save_sem.at[1]),
    ] + [
        pltpu.make_async_copy(ic_buf.at[flip(me, mask, n)], tail_out[k], save_sem.at[2 + k])
        for k, mask in enumerate(masks)
    ]
    for save in saves:
        save.start()

    for d in range(1, replicas):
        source = (rep + d) % replicas
        pltpu.make_async_remote_copy(
            src_ref=mine.at[source],
            dst_ref=sync_out.at[source],
            send_sem=g_send.at[d],
            recv_sem=g_recv.at[source],
            device_id={"replica": source},
            device_id_type=MESH,
        ).wait_recv()
        f_copy(d).wait_send()
        g_copy(d).wait_send()
    for d in range(1, n):
        tok_copy(d).wait_send()
    for s in range(chips - 1):

        @pl.when(goes_right(s))
        def _(s=s):
            right(s).wait_send()

        @pl.when(goes_left(s))
        def _(s=s):
            left(s).wait_send()

    for j in range(chips):
        beside(j).wait_send()
    keep_cols.wait()
    for save in saves:
        save.wait()
    for mask in range(1, n):
        x_copy(mask).wait_send()
        source = flip(me, mask, n)
        pltpu.make_async_remote_copy(
            src_ref=own_cols,
            dst_ref=cols_out.at[source],
            send_sem=x_send.at[mask],
            recv_sem=x_recv.at[source],
            device_id={"fsdp": source},
            device_id_type=MESH,
        ).wait_recv()
    for mask in far + near:
        ic_copy(mask).wait_send()
        source = flip(me, mask, n)
        pltpu.make_async_remote_copy(
            src_ref=ic_buf.at[source],
            dst_ref=ic_out.at[:, span_of(source)],
            send_sem=ic_send.at[mask],
            recv_sem=ic_recv.at[mask],
            device_id={"fsdp": source},
            device_id_type=MESH,
        ).wait_recv()


def on_device(
    token_ids,
    inputs,
    key_cotangent,
    key_weight,
    adam_m,
    adam_v,
    frag_local,
    frag_global,
    outer_mom,
    owner,
    fragment,
):
    tokens = inputs.shape[0]
    rows, width = key_weight.shape[1:]
    slots, _, frag_width = frag_local.shape[1:]
    n = lax.axis_size("fsdp")
    replicas = lax.axis_size("replica")
    seq_len = tokens * n
    quarter = rows // replicas
    tok = token_ids[None, :]
    anywhere = pl.BlockSpec(memory_space=pl.ANY)
    smem = pl.BlockSpec(memory_space=pltpu.SMEM)
    vmem = pl.BlockSpec(memory_space=pltpu.VMEM)
    hbm = pl.BlockSpec(memory_space=pltpu.HBM)
    dma = pltpu.SemaphoreType.DMA
    chips = n // 2
    bf16, f32 = jnp.bfloat16, jnp.float32
    masks = tail_masks(n)
    columns, key_grad, total, near_grad, *last = pl.pallas_call(
        functools.partial(exchange, n, replicas),
        out_shape=(
            jax.ShapeDtypeStruct((n, tokens, rows), bf16),
            jax.ShapeDtypeStruct((n, tokens, width), bf16),
            jax.ShapeDtypeStruct((replicas, quarter, frag_width), bf16),
            jax.ShapeDtypeStruct((tokens, n * rows), bf16),
        )
        + (jax.ShapeDtypeStruct((tokens, rows), bf16),) * len(masks),
        in_specs=[smem, smem, hbm, hbm] + [anywhere] * 5,
        out_specs=(anywhere, hbm, vmem, hbm) + (hbm,) * len(masks),
        scratch_shapes=[
            pltpu.VMEM((n, tokens, width), bf16),
            pltpu.VMEM((n, 1, tokens), jnp.int32),
            pltpu.VMEM((n, tokens, width), bf16),
            pltpu.VMEM((n, tokens, rows), bf16),
            pltpu.VMEM((rows, width), f32),
            pltpu.VMEM((rows, width), bf16),
            pltpu.VMEM((slots, rows, frag_width), f32),
            pltpu.VMEM((rows, frag_width), f32),
            pltpu.VMEM((rows, frag_width), f32),
            pltpu.VMEM((replicas, quarter, frag_width), bf16),
            pltpu.VMEM((replicas, quarter, frag_width), bf16),
            pltpu.VMEM((tokens, rows), bf16),
            dma((7,)),
            dma((2 + len(masks),)),
            dma((n,)),
            dma((n,)),
            dma((chips,)),
            dma((chips,)),
            dma((chips,)),
            dma((n,)),
            dma((n,)),
            dma((n,)),
            dma((n,)),
            dma((n,)),
            dma((replicas,)),
            dma((replicas,)),
            dma((replicas,)),
            dma((replicas,)),
        ],
        compiler_params=pltpu.CompilerParams(
            collective_id=0, has_side_effects=True, vmem_limit_bytes=63 * 1024 * 1024
        ),
    )(
        owner,
        fragment,
        tok,
        key_cotangent,
        inputs,
        key_weight[0],
        frag_local[0],
        frag_global[0],
        outer_mom[0],
    )
    last = [
        lax.ppermute(block, "fsdp", [(i, i ^ mask) for i in range(n)])
        for block, mask in zip(last, masks)
    ]
    size = tokens * n * rows * 2
    grad = jax.ShapeDtypeStruct((tokens, n * rows), bf16)
    input_cotangent = pl.pallas_call(
        functools.partial(through, n),
        out_shape=grad,
        in_specs=[anywhere],
        out_specs=anywhere,
        scratch_shapes=[pltpu.VMEM((tokens, n * rows), bf16), dma((n,)), dma((n,))],
        cost_estimate=pl.CostEstimate(flops=0, bytes_accessed=2 * size, transcendentals=0),
    )(near_grad)
    if masks:
        input_cotangent = pl.pallas_call(
            functools.partial(put_last, n),
            out_shape=grad,
            in_specs=[anywhere] * (1 + len(masks)),
            out_specs=anywhere,
            scratch_shapes=[dma((len(masks),))],
            input_output_aliases={0: 0},
        )(input_cotangent, *[pltpu.with_memory_space_constraint(block, pltpu.VMEM) for block in last])
    weight_sum = lax.dot_general(
        columns.reshape(seq_len, rows),
        key_grad.reshape(seq_len, width),
        (((0,), (0,)), ((), ())),
        preferred_element_type=f32,
    )
    weight_grad = (weight_sum / seq_len)[None]
    moment_mean = beta_one * adam_m + (1.0 - beta_one) * weight_grad
    moment_square = beta_two * adam_v + (1.0 - beta_two) * weight_grad * weight_grad
    mean_hat = moment_mean / (1.0 - beta_one**adam_step)
    square_hat = moment_square / (1.0 - beta_two**adam_step)
    new_weight = key_weight - adam_lr * (
        mean_hat / (jnp.sqrt(square_hat) + adam_eps) + weight_decay * key_weight
    )
    is_owner = lax.axis_index("replica") == owner[0]
    synced = total.reshape(1, rows, frag_width).astype(f32)
    outer_grad = (
        frag_global - (outer_lr * outer_momentum * outer_momentum) * outer_mom - synced
    ) / (outer_lr * (1.0 + outer_momentum))
    new_outer_mom = jnp.where(is_owner, outer_momentum * outer_mom + outer_grad, outer_mom)
    return (input_cotangent, new_weight, moment_mean, moment_square, synced, new_outer_mom)


def solution(mesh):
    in_specs = (
        P(("replica", "fsdp")),
        P(("replica", "fsdp"), None),
        P(("replica", "fsdp"), None),
        P("replica", "fsdp", None),
        P("replica", "fsdp", None),
        P("replica", "fsdp", None),
        P("replica", None, "fsdp", None),
        P("replica", "fsdp", None),
        P("replica", "fsdp", None),
        P("fsdp"),
        P("replica"),
    )
    out_specs = (
        P(("replica", "fsdp"), None),
        P("replica", "fsdp", None),
        P("replica", "fsdp", None),
        P("replica", "fsdp", None),
        P("replica", "fsdp", None),
        P("replica", "fsdp", None),
    )
    return jax.shard_map(
        on_device, mesh=mesh, in_specs=in_specs, out_specs=out_specs, check_vma=False
    )
```

```python
import functools
import math

import jax
import jax.numpy as jnp
from jax import lax
from jax.experimental import pallas as pl
from jax.experimental.pallas import tpu as pltpu
from jax.sharding import PartitionSpec as P

HEAD = 128


begin_token = 128000
rope_base = 500000.0
beta_one = 0.9
beta_two = 0.95
adam_lr = 0.001
adam_eps = 1e-08
adam_step = 10.0
weight_decay = 0.1
outer_lr = 0.7
outer_momentum = 0.9


MESH = pl.DeviceIdType.MESH


def flip(index, mask, size):
    total, bit = 0, 1
    while bit < size:
        own, other = (index // bit) % 2, (mask // bit) % 2
        total = total + bit * (own + other - 2 * own * other)
        bit *= 2
    return total


def tail_masks(n):
    return [n // 2 + 1, n - 1] if n > 4 else []


def through(n, blocks_ref, out_ref, held, in_sem, out_sem):
    rows = blocks_ref.shape[1] // n
    spans = [slice(j * rows, (j + 1) * rows) for j in range(n)]
    arrive = [
        pltpu.make_async_copy(blocks_ref.at[:, at], held.at[:, at], in_sem.at[j])
        for j, at in enumerate(spans)
    ]
    leave = [
        pltpu.make_async_copy(held.at[:, at], out_ref.at[:, at], out_sem.at[j])
        for j, at in enumerate(spans)
    ]
    for copy in arrive:
        copy.start()
    for j in range(n):
        arrive[j].wait()
        leave[j].start()
    for copy in leave:
        copy.wait()


def put_last(n, *refs):
    masks = tail_masks(n)
    blocks, out_ref, sem = refs[1 : 1 + len(masks)], refs[-2], refs[-1]
    me = lax.axis_index("fsdp")
    rows = blocks[0].shape[1]
    copies = []
    for k, mask in enumerate(masks):
        at = pl.ds(pl.multiple_of(flip(me, mask, n) * rows, rows), rows)
        copies.append(pltpu.make_async_copy(blocks[k], out_ref.at[:, at], sem.at[k]))
    for copy in copies:
        copy.start()
    for copy in copies:
        copy.wait()


def exchange(
    n,
    replicas,
    owner_ref,
    fragment_ref,
    tok_ref,
    kc_hbm,
    x_hbm,
    w_hbm,
    local_hbm,
    global_hbm,
    mom_hbm,
    *rest,
):
    masks = tail_masks(n)
    cols_out, kg_out, sync_out, ic_out = rest[:4]
    tail_out, rest = rest[4 : 4 + len(masks)], rest[4 + len(masks) :]
    (
        kc_all,
        tok_all,
        kg_buf,
        ic_buf,
        w_buf,
        w_bf,
        local_buf,
        global_buf,
        mom_buf,
        mine,
        parts,
        own_cols,
        load_sem,
        save_sem,
        tok_send,
        tok_recv,
        kc_send_right,
        kc_send_left,
        kc_send_side,
        kc_recv,
        x_send,
        x_recv,
        ic_send,
        ic_recv,
        f_send,
        f_recv,
        g_send,
        g_recv,
    ) = rest
    me = lax.axis_index("fsdp")
    rep = lax.axis_index("replica")
    chips = n // 2
    chip, core = me // 2, me % 2
    side = me + 1 - 2 * core
    tokens, width = kc_hbm.shape
    rows = w_hbm.shape[0]
    quarter = rows // replicas
    step_rows = min(32, quarter)

    barrier = pltpu.get_barrier_semaphore()
    for d in range(1, n):
        pl.semaphore_signal(
            barrier, inc=1, device_id={"fsdp": (me + d) % n}, device_id_type=MESH
        )
    for d in range(1, replicas):
        pl.semaphore_signal(
            barrier, inc=1, device_id={"replica": (rep + d) % replicas}, device_id_type=MESH
        )

    loads = [
        pltpu.make_async_copy(local_hbm, local_buf, load_sem.at[0]),
        pltpu.make_async_copy(global_hbm, global_buf, load_sem.at[1]),
        pltpu.make_async_copy(mom_hbm, mom_buf, load_sem.at[2]),
        pltpu.make_async_copy(kc_hbm, kc_all.at[me], load_sem.at[3]),
        pltpu.make_async_copy(tok_ref, tok_all.at[me], load_sem.at[4]),
        pltpu.make_async_copy(
            x_hbm.at[:, pl.ds(pl.multiple_of(me * rows, rows), rows)], own_cols, load_sem.at[5]
        ),
        pltpu.make_async_copy(w_hbm, w_buf, load_sem.at[6]),
    ]
    for load in loads:
        load.start()
    pl.semaphore_wait(barrier, n - 1 + replicas - 1)

    def tok_copy(d):
        return pltpu.make_async_remote_copy(
            src_ref=tok_ref,
            dst_ref=tok_all.at[me],
            send_sem=tok_send.at[d],
            recv_sem=tok_recv.at[me],
            device_id={"fsdp": (me + d) % n},
            device_id_type=MESH,
        )

    def kc_copy(block, target, send_sem, first=False):
        return pltpu.make_async_remote_copy(
            src_ref=kc_hbm if first else kc_all.at[block],
            dst_ref=kc_all.at[block],
            send_sem=send_sem,
            recv_sem=kc_recv.at[block],
            device_id={"fsdp": target},
            device_id_type=MESH,
        )

    def block_of(at_chip):
        return jnp.clip(at_chip, 0, chips - 1) * 2 + core

    def right(s):
        target = jnp.minimum(me + 2, n - 1)
        return kc_copy(block_of(chip - s), target, kc_send_right.at[s], s == 0)

    def left(s):
        target = jnp.maximum(me - 2, 0)
        return kc_copy(block_of(chip + s), target, kc_send_left.at[s], s == 0)

    def goes_right(s):
        return jnp.logical_and(chip - s >= 0, chip + 1 < chips)

    def goes_left(s):
        return jnp.logical_and(chip + s < chips, chip >= 1)

    def beside(at_chip, first=False):
        at = jnp.clip(at_chip, 0, chips - 1)
        return kc_copy(at * 2 + core, side, kc_send_side.at[at], first)

    def x_copy(mask, part=slice(None)):
        peer = flip(me, mask, n)
        low, high, _ = part.indices(tokens)
        at = pl.ds(low, high - low)
        return pltpu.make_async_remote_copy(
            src_ref=x_hbm.at[at, span_of(peer)],
            dst_ref=cols_out.at[me, at],
            send_sem=x_send.at[mask],
            recv_sem=x_recv.at[me],
            device_id={"fsdp": peer},
            device_id_type=MESH,
        )

    def span_of(at):
        return pl.ds(pl.multiple_of(at * rows, rows), rows)

    def ic_copy(mask):
        peer = flip(me, mask, n)
        return pltpu.make_async_remote_copy(
            src_ref=ic_buf.at[peer],
            dst_ref=ic_out.at[:, span_of(me)],
            send_sem=ic_send.at[mask],
            recv_sem=ic_recv.at[mask],
            device_id={"fsdp": peer},
            device_id_type=MESH,
        )

    def f_copy(d):
        peer = (rep + d) % replicas
        return pltpu.make_async_remote_copy(
            src_ref=mine.at[peer],
            dst_ref=parts.at[rep],
            send_sem=f_send.at[d],
            recv_sem=f_recv.at[rep],
            device_id={"replica": peer},
            device_id_type=MESH,
        )

    def g_copy(d):
        peer = (rep + d) % replicas
        return pltpu.make_async_remote_copy(
            src_ref=sync_out.at[rep],
            dst_ref=sync_out.at[rep],
            send_sem=g_send.at[d],
            recv_sem=g_recv.at[rep],
            device_id={"replica": peer},
            device_id_type=MESH,
        )

    far = [mask for mask in range(n // 2, n) if mask not in masks]
    near = [mask for mask in range(1, n // 2)]
    near_first = near[1:] + near[:1]
    edge = jnp.logical_or(chip == 0, chip == chips - 1)
    edge_waves = {"first": near + far[-1:], 0: far[-1:] + masks[::-1] + far[:-1]}
    inner_waves = {"first": far[-1:], 0: far[-1:] + masks[::-1] + far[:-1], 1: near}
    head = tokens // 4 // 16 * 16

    def x_wave(event):
        def start(waves):
            for mask in waves[event]:
                if mask != far[-1]:
                    x_copy(mask).start()
                elif event == "first":
                    x_copy(mask, slice(0, head)).start()
                else:
                    x_copy(mask, slice(head, tokens)).start()

        for here, waves in ((edge, edge_waves), (jnp.logical_not(edge), inner_waves)):
            if event in waves:
                pl.when(here)(functools.partial(start, waves))

    @pl.when(goes_right(0))
    def _():
        right(0).start()

    @pl.when(goes_left(0))
    def _():
        left(0).start()

    beside(chip, True).start()
    x_wave("first")
    for d in range(1, n):
        tok_copy(d).start()

    loads[6].wait()

    def round_weight(i, carry):
        at = pl.ds(pl.multiple_of(i * 32, 32), 32)
        w_bf[at, :] = w_buf[at, :].astype(jnp.bfloat16)
        return carry

    lax.fori_loop(0, rows // 32, round_weight, 0)

    def send_term():
        for load in loads[:3]:
            load.wait()
        here = owner_ref[0] == rep
        slot = fragment_ref[0]

        for q in range(replicas):

            def term(i, carry, q=q):
                at = pl.ds(pl.multiple_of(q * quarter + i * step_rows, step_rows), step_rows)
                to = pl.ds(pl.multiple_of(i * step_rows, step_rows), step_rows)
                value = ((1.0 + outer_momentum) * outer_lr / replicas) * local_buf[slot, at, :]
                state = (1.0 - outer_lr * (1.0 + outer_momentum)) * global_buf[at, :] - (
                    outer_lr * outer_momentum * outer_momentum
                ) * mom_buf[at, :]
                value = value + jnp.where(here, state, 0.0)
                mine[q, to, :] = value.astype(jnp.bfloat16)
                return carry

            lax.fori_loop(0, quarter // step_rows, term, 0)
        for d in range(1, replicas):
            f_copy(d).start()

    def share_sums():
        for d in range(1, replicas):
            source = (rep + d) % replicas
            pltpu.make_async_remote_copy(
                src_ref=mine.at[source],
                dst_ref=parts.at[source],
                send_sem=f_send.at[d],
                recv_sem=f_recv.at[source],
                device_id={"replica": source},
                device_id_type=MESH,
            ).wait_recv()

        def add_parts(i, carry):
            to = pl.ds(pl.multiple_of(i * step_rows, step_rows), step_rows)
            total = mine[rep, to, :].astype(jnp.float32)
            for d in range(1, replicas):
                total = total + parts[(rep + d) % replicas, to, :].astype(jnp.float32)
            sync_out[rep, to, :] = total.astype(jnp.bfloat16)
            return carry

        lax.fori_loop(0, quarter // step_rows, add_parts, 0)
        for d in range(1, replicas):
            g_copy(d).start()

    half = HEAD // 2
    lane = lax.broadcasted_iota(jnp.int32, (tokens, HEAD), 1)
    sign = jnp.where(lane < half, 1.0, -1.0)
    exponent = (lax.broadcasted_iota(jnp.int32, (8, HEAD), 1) % half).astype(jnp.float32)
    frequency = jnp.exp(exponent * (-2.0 / HEAD * math.log(rope_base)))[0:1, :]
    row = lax.broadcasted_iota(jnp.int32, (tokens, tokens), 0)
    column = lax.broadcasted_iota(jnp.int32, (tokens, tokens), 1)

    def one_block(k):
        b = flip(me, k, n)

        def latest_of(j, latest):
            is_start = jnp.broadcast_to(tok_all[j], (tokens, tokens)) == begin_token
            at = j * tokens + column
            kept = jnp.where(
                jnp.logical_and(is_start, at <= b * tokens + row), at.astype(jnp.float32), -1.0
            )
            return jnp.maximum(latest, kept)

        latest = lax.fori_loop(0, n, latest_of, jnp.full((tokens, tokens), -1.0, jnp.float32))
        latest = jnp.max(latest, axis=1, keepdims=True)
        here_at = (b * tokens + lax.broadcasted_iota(jnp.int32, (tokens, HEAD), 0)).astype(
            jnp.float32
        )
        angles = (here_at - latest) * frequency
        cosine = jnp.cos(angles)
        sine = jnp.sin(angles) * sign
        for h in range(width // HEAD):
            at = slice(h * HEAD, (h + 1) * HEAD)
            value = kc_all[b, :, at].astype(jnp.float32)
            turned = value * cosine + pltpu.roll(value, half, 1) * sine
            kg_buf[b, :, at] = turned.astype(jnp.bfloat16)
        ic_buf[b] = lax.dot_general(
            kg_buf[b], w_bf[...], (((1,), (1,)), ((), ())), preferred_element_type=jnp.float32
        ).astype(jnp.bfloat16)

    def block_step(k, carry):
        @pl.when(k % 2 == 1)
        def _():
            kc_copy(flip(me, k, n), side, kc_send_side.at[0]).wait_recv()

        one_block(k)
        sent = k > 0
        for last in masks:
            sent = jnp.logical_and(sent, k != last)

        @pl.when(sent)
        def _():
            ic_copy(k).start()

        return carry

    def near_blocks():
        for load in loads[3:5]:
            load.wait()
        for d in range(1, n):
            source = (me + d) % n
            pltpu.make_async_remote_copy(
                src_ref=tok_ref,
                dst_ref=tok_all.at[source],
                send_sem=tok_send.at[d],
                recv_sem=tok_recv.at[source],
                device_id={"fsdp": source},
                device_id_type=MESH,
            ).wait_recv()
        lax.fori_loop(0, n // 2, block_step, 0)

    def far_step(j, carry):
        k = n // 2 + 2 * (j % (n // 4)) + j // (n // 4)
        return block_step(k, carry)

    for s in range(chips - 1):
        if s == chips - 2:
            near_blocks()

        @pl.when(chip - 1 - s >= 0)
        def _(s=s):
            block = chip - 1 - s
            kc_copy(block_of(block), side, kc_send_side.at[0]).wait_recv()

            @pl.when(goes_right(s + 1))
            def _():
                right(s + 1).start()

            beside(block).start()

        @pl.when(chip + 1 + s < chips)
        def _(s=s):
            block = chip + 1 + s
            kc_copy(block_of(block), side, kc_send_side.at[0]).wait_recv()

            @pl.when(goes_left(s + 1))
            def _():
                left(s + 1).start()

            beside(block).start()

        x_wave(s)
        if s == 0:
            send_term()
        if s == min(1, chips - 2):
            share_sums()
    lax.fori_loop(0, n // 2, far_step, 0)
    loads[5].wait()
    keep_cols = pltpu.make_async_copy(own_cols, cols_out.at[me], load_sem.at[0])
    keep_cols.start()

    saves = [
        pltpu.make_async_copy(kg_buf, kg_out, save_sem.at[0]),
        pltpu.make_async_copy(ic_buf.at[me], ic_out.at[:, span_of(me)], save_sem.at[1]),
    ] + [
        pltpu.make_async_copy(ic_buf.at[flip(me, mask, n)], tail_out[k], save_sem.at[2 + k])
        for k, mask in enumerate(masks)
    ]
    for save in saves:
        save.start()

    for d in range(1, replicas):
        source = (rep + d) % replicas
        pltpu.make_async_remote_copy(
            src_ref=mine.at[source],
            dst_ref=sync_out.at[source],
            send_sem=g_send.at[d],
            recv_sem=g_recv.at[source],
            device_id={"replica": source},
            device_id_type=MESH,
        ).wait_recv()
        f_copy(d).wait_send()
        g_copy(d).wait_send()
    for d in range(1, n):
        tok_copy(d).wait_send()
    for s in range(chips - 1):

        @pl.when(goes_right(s))
        def _(s=s):
            right(s).wait_send()

        @pl.when(goes_left(s))
        def _(s=s):
            left(s).wait_send()

    for j in range(chips):
        beside(j).wait_send()
    keep_cols.wait()
    for save in saves:
        save.wait()
    for mask in range(1, n):
        x_copy(mask).wait_send()
        source = flip(me, mask, n)
        pltpu.make_async_remote_copy(
            src_ref=own_cols,
            dst_ref=cols_out.at[source],
            send_sem=x_send.at[mask],
            recv_sem=x_recv.at[source],
            device_id={"fsdp": source},
            device_id_type=MESH,
        ).wait_recv()
    for mask in far + near:
        ic_copy(mask).wait_send()
        source = flip(me, mask, n)
        pltpu.make_async_remote_copy(
            src_ref=ic_buf.at[source],
            dst_ref=ic_out.at[:, span_of(source)],
            send_sem=ic_send.at[mask],
            recv_sem=ic_recv.at[mask],
            device_id={"fsdp": source},
            device_id_type=MESH,
        ).wait_recv()


def on_device(
    token_ids,
    inputs,
    key_cotangent,
    key_weight,
    adam_m,
    adam_v,
    frag_local,
    frag_global,
    outer_mom,
    owner,
    fragment,
):
    tokens = inputs.shape[0]
    rows, width = key_weight.shape[1:]
    slots, _, frag_width = frag_local.shape[1:]
    n = lax.axis_size("fsdp")
    replicas = lax.axis_size("replica")
    seq_len = tokens * n
    quarter = rows // replicas
    tok = token_ids[None, :]
    anywhere = pl.BlockSpec(memory_space=pl.ANY)
    smem = pl.BlockSpec(memory_space=pltpu.SMEM)
    vmem = pl.BlockSpec(memory_space=pltpu.VMEM)
    hbm = pl.BlockSpec(memory_space=pltpu.HBM)
    dma = pltpu.SemaphoreType.DMA
    chips = n // 2
    bf16, f32 = jnp.bfloat16, jnp.float32
    masks = tail_masks(n)
    columns, key_grad, total, near_grad, *last = pl.pallas_call(
        functools.partial(exchange, n, replicas),
        out_shape=(
            jax.ShapeDtypeStruct((n, tokens, rows), bf16),
            jax.ShapeDtypeStruct((n, tokens, width), bf16),
            jax.ShapeDtypeStruct((replicas, quarter, frag_width), bf16),
            jax.ShapeDtypeStruct((tokens, n * rows), bf16),
        )
        + (jax.ShapeDtypeStruct((tokens, rows), bf16),) * len(masks),
        in_specs=[smem, smem, hbm, hbm] + [anywhere] * 5,
        out_specs=(anywhere, hbm, vmem, hbm) + (hbm,) * len(masks),
        scratch_shapes=[
            pltpu.VMEM((n, tokens, width), bf16),
            pltpu.VMEM((n, 1, tokens), jnp.int32),
            pltpu.VMEM((n, tokens, width), bf16),
            pltpu.VMEM((n, tokens, rows), bf16),
            pltpu.VMEM((rows, width), f32),
            pltpu.VMEM((rows, width), bf16),
            pltpu.VMEM((slots, rows, frag_width), f32),
            pltpu.VMEM((rows, frag_width), f32),
            pltpu.VMEM((rows, frag_width), f32),
            pltpu.VMEM((replicas, quarter, frag_width), bf16),
            pltpu.VMEM((replicas, quarter, frag_width), bf16),
            pltpu.VMEM((tokens, rows), bf16),
            dma((7,)),
            dma((2 + len(masks),)),
            dma((n,)),
            dma((n,)),
            dma((chips,)),
            dma((chips,)),
            dma((chips,)),
            dma((n,)),
            dma((n,)),
            dma((n,)),
            dma((n,)),
            dma((n,)),
            dma((replicas,)),
            dma((replicas,)),
            dma((replicas,)),
            dma((replicas,)),
        ],
        compiler_params=pltpu.CompilerParams(
            collective_id=0, has_side_effects=True, vmem_limit_bytes=63 * 1024 * 1024
        ),
    )(
        owner,
        fragment,
        tok,
        key_cotangent,
        inputs,
        key_weight[0],
        frag_local[0],
        frag_global[0],
        outer_mom[0],
    )
    last = [
        lax.ppermute(block, "fsdp", [(i, i ^ mask) for i in range(n)])
        for block, mask in zip(last, masks)
    ]
    size = tokens * n * rows * 2
    grad = jax.ShapeDtypeStruct((tokens, n * rows), bf16)
    input_cotangent = pl.pallas_call(
        functools.partial(through, n),
        out_shape=grad,
        in_specs=[anywhere],
        out_specs=anywhere,
        scratch_shapes=[pltpu.VMEM((tokens, n * rows), bf16), dma((n,)), dma((n,))],
        cost_estimate=pl.CostEstimate(flops=0, bytes_accessed=2 * size, transcendentals=0),
    )(near_grad)
    if masks:
        input_cotangent = pl.pallas_call(
            functools.partial(put_last, n),
            out_shape=grad,
            in_specs=[anywhere] * (1 + len(masks)),
            out_specs=anywhere,
            scratch_shapes=[dma((len(masks),))],
            input_output_aliases={0: 0},
        )(input_cotangent, *[pltpu.with_memory_space_constraint(block, pltpu.VMEM) for block in last])
    weight_sum = lax.dot_general(
        columns.reshape(seq_len, rows),
        key_grad.reshape(seq_len, width),
        (((0,), (0,)), ((), ())),
        preferred_element_type=f32,
    )
    weight_grad = (weight_sum / seq_len)[None]
    moment_mean = beta_one * adam_m + (1.0 - beta_one) * weight_grad
    moment_square = beta_two * adam_v + (1.0 - beta_two) * weight_grad * weight_grad
    mean_hat = moment_mean / (1.0 - beta_one**adam_step)
    square_hat = moment_square / (1.0 - beta_two**adam_step)
    new_weight = key_weight - adam_lr * (
        mean_hat / (jnp.sqrt(square_hat) + adam_eps) + weight_decay * key_weight
    )
    is_owner = lax.axis_index("replica") == owner[0]
    synced = total.reshape(1, rows, frag_width).astype(f32)
    outer_grad = (
        frag_global - (outer_lr * outer_momentum * outer_momentum) * outer_mom - synced
    ) / (outer_lr * (1.0 + outer_momentum))
    new_outer_mom = jnp.where(is_owner, outer_momentum * outer_mom + outer_grad, outer_mom)
    return (input_cotangent, new_weight, moment_mean, moment_square, synced, new_outer_mom)


def solution(mesh):
    in_specs = (
        P(("replica", "fsdp")),
        P(("replica", "fsdp"), None),
        P(("replica", "fsdp"), None),
        P("replica", "fsdp", None),
        P("replica", "fsdp", None),
        P("replica", "fsdp", None),
        P("replica", None, "fsdp", None),
        P("replica", "fsdp", None),
        P("replica", "fsdp", None),
        P("fsdp"),
        P("replica"),
    )
    out_specs = (
        P(("replica", "fsdp"), None),
        P("replica", "fsdp", None),
        P("replica", "fsdp", None),
        P("replica", "fsdp", None),
        P("replica", "fsdp", None),
        P("replica", "fsdp", None),
    )
    return jax.shard_map(
        on_device, mesh=mesh, in_specs=in_specs, out_specs=out_specs, check_vma=False
    )
```
